128 devices in a mesh: row: 4 (over y), col: 16 (over z, x_hi, core), tm: 2 (over x_lo).
Axes of the slice: x: 4 (x_hi: 2, x_lo: 2; x = x_hi * 2 + x_lo), y: 4, z: 4, core: 2. Of those that a mesh axis runs over, the one named last changes fastest.
Arguments:
- counts: float32 [1024, 1024, 512], P('row', 'col', 'tm'), may hold values from 0 to 60, as said below
- factor_a: float32 [1024, 32], P('row'), may hold values from 0.05 to 1
- factor_b: float32 [1024, 32], P(('col', 'tm')), may hold values from 0.05 to 3, as said below
- factor_c: float32 [512, 32], P('tm'), may hold values from 0.1 to 1
Outputs:
- updated_a: float32 [1024, 32], P(('row', 'col', 'tm'))
The draws below stay inside these ranges and needn't reach their ends.
Inputs may be any that keep to these rules, and one draw needn't show every extreme that they name: `counts`: whole numbers. `factor_b`: positive.
All inputs are finite; a program needn't handle non-finite values.
Results may differ from the reference program's by a relative error of at most 0.00027.
Values sent between devices are 32-bit elements; how exact they have to be, the bound alone decides.
No kernel may reach another device: no remote copies, remote signals or barrier semaphores. Data moves between devices by JAX's collectives and lax.ppermute only.
A program may use at most 128 MiB of HBM per device.

```python
import math
import jax
import jax.numpy as jnp
from jax import lax

R = 32
ITERS = 6
I = 1024
J = 1024
K = 512


def sparse_levels(key_live, key_level, length, highest, chance):
    active = jax.random.randint(key_live, (length, R), 0, chance) == 0
    levels = jax.random.randint(key_level, (length, R), 1, highest + 1)
    return jnp.where(active, levels, 0).astype(jnp.int32)


def draw_counts(key, part):
    subkeys = jax.random.split(key, 7)
    rows_star = sparse_levels(subkeys[0], subkeys[1], I, 4, 4)
    cols_star = sparse_levels(subkeys[2], subkeys[3], J, 4, 4)
    bins_star = sparse_levels(subkeys[4], subkeys[5], K, 8, 8)
    paired = (rows_star[:, None, :] * cols_star[None, :, :]).reshape(I * J, R)
    planted = jnp.dot(paired, bins_star.T, preferred_element_type=jnp.int32).reshape(I, J, K)
    jitter = jax.random.randint(subkeys[6], (I, J, K), 0, 3)
    return jnp.minimum(planted + jitter, 60).astype(jnp.float32)


def draw_factor_b(key, part):
    rise = 1.0 + 2.0 * jnp.arange(J, dtype=jnp.float32)[:, None] / max(J - 1, 1)
    base = jnp.exp(jax.random.uniform(key, (J, R), jnp.float32, jnp.log(0.1), 0.0))
    return (base * rise).astype(jnp.float32)


def level_of(key, shape, cuts, least, largest):
    def one(axis_at, blocks):
        heights = jax.random.uniform(jax.random.fold_in(jax.random.fold_in(key, 6), axis_at), (blocks,), jnp.float32, least / len(cuts), largest / len(cuts))
        return jnp.repeat(jnp.exp(heights), shape[axis_at] // blocks).reshape((-1,) + (1,) * (len(shape) - axis_at - 1))

    factor_of = one(*cuts[0])
    for cut in cuts[1:]:
        factor_of = factor_of * one(*cut)
    return factor_of


def setup_inputs(seed: int = 0) -> dict:
    splits = jax.random.split(jax.random.key(seed), 5)
    counts = draw_counts(jax.random.fold_in(splits[4], 71), 0)
    factor_a = jnp.clip(jnp.exp(math.log(1.0) - 2.9957323 * jax.random.uniform(splits[1], (I, R), jnp.float32) ** level_of(splits[1], (I, R), ((0, 4),), -0.2, 0.2)), 0.05, 1.0)
    factor_b = draw_factor_b(jax.random.fold_in(splits[4], 71), 0)
    factor_c = jnp.clip(jnp.exp(math.log(1.0) - 2.3025851 * jax.random.uniform(splits[3], (K, R), jnp.float32) ** level_of(splits[3], (K, R), ((0, 2),), -0.2, 0.2)), 0.1, 1.0)
    return {"counts": counts, "factor_a": factor_a, "factor_b": factor_b, "factor_c": factor_c}


def reference(counts, factor_a, factor_b, factor_c):
    sum_b = jnp.sum(factor_b, axis=0)
    sum_c = jnp.sum(factor_c, axis=0)
    norm_b = factor_b / (sum_b / J)
    norm_c = factor_c / (sum_c / K)
    kr = (norm_b.T[:, :, None] * norm_c.T[:, None, :]).reshape(R, J * K)
    flat = counts.reshape(I, J * K)
    block = math.gcd(I, 64)

    def one_block(pair):
        rows, weights = pair
        model = jnp.dot(weights, kr, precision=lax.Precision.HIGHEST, preferred_element_type=jnp.float32)
        ratio = rows / model
        total = lax.dot_general(ratio, kr, (((1,), (1,)), ((), ())), precision=lax.Precision.HIGHEST, preferred_element_type=jnp.float32)
        return total / float(J * K)

    current = factor_a
    for step in range(ITERS):
        phi = lax.map(one_block, (flat.reshape(I // block, block, J * K), current.reshape(I // block, block, R)))
        current = current * phi.reshape(I, R)
    return current
```

```python
import functools

import jax
import jax.numpy as jnp
from jax import lax
from jax.experimental import pallas as pl
from jax.experimental.pallas import tpu as pltpu
from jax.sharding import PartitionSpec as P

R = 32
ITERS = 6
LANES = 128
FOLD = LANES // R


def halves(x):
    high = x.astype(jnp.bfloat16)
    low = (x - high.astype(jnp.float32)).astype(jnp.bfloat16)
    return high, low


def pack(x):
    n = x.shape[0] // FOLD
    return jnp.concatenate([x[g * n : (g + 1) * n] for g in range(FOLD)], axis=1)


def step_kernel(sub, unroll, cur_ref, b_ref, w1_ref, w2_ref, n_ref, out_ref, rep_ref, tot_ref):
    step = pl.program_id(0)
    rows, cols, bins = n_ref.shape
    quarter = cur_ref.shape[0]
    group = lax.broadcasted_iota(jnp.int32, (quarter, LANES), 1) // R

    @pl.when(step == 0)
    def _():
        x = cur_ref[...]
        turned = [x] + [pltpu.roll(x, R * g, 1) for g in range(1, FOLD)]
        for g in range(FOLD):
            y = turned[(0 - g) % FOLD]
            for at in range(1, FOLD):
                y = jnp.where(group == at, turned[(at - g) % FOLD], y)
            rep_ref[pl.ds(g * quarter, quarter), :] = y

    b = b_ref[...]
    w1 = w1_ref[...]
    w2 = w2_ref[...]
    odd = (lax.broadcasted_iota(jnp.int32, (sub * cols, LANES), 1) // R) % 2 == 1

    def body(s, carry):
        at = step * rows + s * sub
        weights = rep_ref[pl.ds(pl.multiple_of(at, sub), sub), :]
        product = (weights[:, None, :] * b[None, :, :]).reshape(sub * cols, LANES)
        high = product.astype(jnp.bfloat16).astype(jnp.float32)
        left = jnp.where(odd, product - high, product).astype(jnp.bfloat16)
        model = jnp.dot(left, w1, preferred_element_type=jnp.float32)
        n = n_ref[pl.ds(pl.multiple_of(s * sub, sub), sub)].reshape(sub * cols, bins)
        near = pl.reciprocal(model, approx=True)
        near = near * (2.0 - model * near)
        ratio = n * near
        high, low = halves(ratio)
        u = jnp.dot(high, w2, preferred_element_type=jnp.float32) + jnp.dot(
            low, w2, preferred_element_type=jnp.float32
        )
        tot_ref[pl.ds(pl.multiple_of(at, sub), sub), :] = jnp.sum(
            u.reshape(sub, cols, LANES) * b[None], axis=1
        )
        return carry

    lax.fori_loop(0, rows // sub, body, 0, unroll=unroll)

    @pl.when(step == pl.num_programs(0) - 1)
    def _():
        y = None
        for g in range(FOLD):
            t = tot_ref[pl.ds(g * quarter, quarter), :]
            t = t + pltpu.roll(t, LANES - R, 1)
            t = pltpu.roll(t, R * g, 1) if g else t
            y = jnp.where(group == g, t, y) if g else t
        out_ref[...] = y


def one_step(cur, b4, w1, w2, counts, rows=32, sub=8, unroll=2):
    whole = lambda shape: pl.BlockSpec(shape, lambda s: (0,) * len(shape))
    n_rows, cols, bins = counts.shape
    return pl.pallas_call(
        functools.partial(step_kernel, sub, unroll),
        grid=(n_rows // rows,),
        in_specs=[
            whole(cur.shape),
            whole(b4.shape),
            whole(w1.shape),
            whole(w2.shape),
            pl.BlockSpec((rows, cols, bins), lambda s: (s, 0, 0)),
        ],
        out_specs=whole(cur.shape),
        out_shape=jax.ShapeDtypeStruct(cur.shape, jnp.float32),
        scratch_shapes=[
            pltpu.VMEM((n_rows, LANES), jnp.float32),
            pltpu.VMEM((n_rows, LANES), jnp.float32),
        ],
        compiler_params=pltpu.CompilerParams(dimension_semantics=("arbitrary",)),
    )(cur, b4, w1, w2, counts)


AXES = ("col", "tm")


def z_turn(k):
    return lambda i: ((i // 8 + k) % 4) * 8 + i % 8


def x_turn(k):
    def to(i):
        z, high, core, low = i // 8, i // 4 % 2, i // 2 % 2, i % 2
        x = (high * 2 + low + k) % 4
        return z * 8 + (x // 2) * 4 + core * 2 + x % 2

    return to


def send(x, to):
    return lax.ppermute(x, AXES, [(i, to(i)) for i in range(32)])


def total(x):
    pairs = [[2 * i, 2 * i + 1] for i in range(8)]
    both = lax.all_gather(x, "col", axis=0, axis_index_groups=pairs)
    x = both[0] + both[1]
    for turn in (z_turn, x_turn):
        got = [send(x, turn(k)) for k in (2, 1, 3)]
        x = (x + got[0]) + (got[1] + got[2])
    return x


def per_device(counts, factor_a, factor_b, factor_c):
    col_count = lax.axis_size("col")
    tm_count = lax.axis_size("tm")
    groups = col_count * tm_count
    whole_j = factor_b.shape[0] * groups
    whole_k = factor_c.shape[0] * tm_count
    cells = float(whole_j * whole_k)
    own = jnp.concatenate(
        [jnp.sum(factor_b, axis=0), jnp.sum(factor_c, axis=0) * (1.0 / col_count)]
    )
    sums = jnp.sum(
        lax.all_to_all(
            jnp.broadcast_to(jnp.tile(own, 2)[None], (groups, LANES)), AXES, 0, 0, tiled=True
        ),
        axis=0,
    )
    other = send(factor_b, lambda i: i ^ 1)
    first = lax.axis_index("tm") == 0
    b_local = jnp.concatenate(
        [jnp.where(first, factor_b, other), jnp.where(first, other, factor_b)], axis=0
    )
    b4 = jnp.tile(b_local, (1, FOLD))
    c_high, c_low = halves(factor_c)
    none = jnp.zeros_like(c_high)
    w1 = jnp.concatenate([c_high.T, c_high.T, c_low.T, c_low.T], axis=0)
    w2 = jnp.concatenate([c_high, c_low, none, none], axis=1)
    scale = jnp.tile(cells / (sums[:R] * sums[R : 2 * R]), FOLD)[None]
    cur = pack(factor_a) * scale
    for step in range(ITERS):
        t = total(one_step(cur, b4, w1, w2, counts))
        cur = cur * (t * (scale / cells if step < ITERS - 1 else 1.0 / cells))
    own_rows = counts.shape[0] // groups
    position = lax.axis_index(AXES)
    per_block = cur.shape[0] // own_rows
    return lax.dynamic_slice(
        cur, ((position % per_block) * own_rows, (position // per_block) * R), (own_rows, R)
    )


def solution(mesh):
    return jax.shard_map(
        per_device,
        mesh=mesh,
        in_specs=(P("row", "col", "tm"), P("row", None), P(("col", "tm"), None), P("tm", None)),
        out_specs=P(("row", "col", "tm"), None),
        check_vma=False,
    )
```

```python
import functools

import jax
import jax.numpy as jnp
from jax import lax
from jax.experimental import pallas as pl
from jax.experimental.pallas import tpu as pltpu
from jax.sharding import PartitionSpec as P

R = 32
ITERS = 6
LANES = 128
FOLD = LANES // R


def halves(x):
    high = lax.reduce_precision(x, 8, 7)
    return high.astype(jnp.bfloat16), (x - high).astype(jnp.bfloat16)


def kernel_halves(x):
    high = x.astype(jnp.bfloat16)
    return high, (x - high.astype(jnp.float32)).astype(jnp.bfloat16)


def pack(x):
    n = x.shape[0] // FOLD
    return jnp.concatenate([x[g * n : (g + 1) * n] for g in range(FOLD)], axis=1)


def step(sub, unroll, core_ref, mine_ref, theirs_ref, b_ref, w1_ref, w2_ref, n_ref, rep_ref, tot_ref):
    rows, cols, bins = n_ref.shape
    half = mine_ref.shape[0]
    group = lax.broadcasted_iota(jnp.int32, (half, LANES), 1) // R
    first = core_ref[0] == 0

    mine, theirs = mine_ref[...], theirs_ref[...]
    weights_of = (jnp.where(first, mine, theirs), jnp.where(first, theirs, mine))
    for at_half, x in enumerate(weights_of):
        turned = [x] + [pltpu.roll(x, R * g, 1) for g in range(1, FOLD)]
        for g in range(FOLD):
            y = turned[(0 - g) % FOLD]
            for at in range(1, FOLD):
                y = jnp.where(group == at, turned[(at - g) % FOLD], y)
            rep_ref[pl.ds((2 * g + at_half) * half, half), :] = y

    b = b_ref[...]

    def part(at):
        weights = rep_ref[pl.ds(at, sub), :]
        product = (weights[:, None, :] * b[None, :, :]).reshape(sub * cols, LANES)
        left = jnp.concatenate(kernel_halves(product), axis=1)
        model = jnp.dot(left, w1_ref[...], preferred_element_type=jnp.float32)
        n = n_ref[pl.ds(at, sub)].reshape(sub * cols, bins)
        near = pl.reciprocal(model, approx=True)
        near = near * (2.0 - model * near)
        high, low = kernel_halves(n * near)
        w2 = w2_ref[...]
        u = jnp.dot(high, w2, preferred_element_type=jnp.float32) + jnp.dot(
            low, w2, preferred_element_type=jnp.float32
        )
        tot_ref[pl.ds(at, sub), :] = jnp.sum(u.reshape(sub, cols, LANES) * b[None], axis=1)

    def body(s, carry):
        for i in range(unroll):
            part(pl.multiple_of((s * unroll + i) * sub, sub))
        return carry

    lax.fori_loop(0, rows // (sub * unroll), body, 0)

    sums = []
    for at_half in range(2):
        y = None
        for g in range(FOLD):
            t = tot_ref[pl.ds((2 * g + at_half) * half, half), :]
            t = t + pltpu.roll(t, LANES - R, 1)
            t = pltpu.roll(t, R * g, 1) if g else t
            y = jnp.where(group == g, t, y) if g else t
        sums.append(y)
    return weights_of, sums, first


def write_halves(sums, first, mine_out, theirs_out):
    mine_out[...] = jnp.where(first, sums[0], sums[1])
    theirs_out[...] = jnp.where(first, sums[1], sums[0])


def middle_kernel(sub, unroll, *refs):
    inputs, mine_out, theirs_out, rep_ref, tot_ref = refs[:7], *refs[7:]
    _, sums, first = step(sub, unroll, *inputs, rep_ref, tot_ref)
    write_halves(sums, first, mine_out, theirs_out)


def last_kernel(sub, unroll, *refs):
    inputs, cur_out, sum_out, rep_ref, tot_ref = refs[:7], *refs[7:]
    weights_of, sums, _ = step(sub, unroll, *inputs, rep_ref, tot_ref)
    half = sums[0].shape[0]
    for at_half in range(2):
        rows = pl.ds(at_half * half, half)
        cur_out[rows, :] = weights_of[at_half]
        sum_out[rows, :] = sums[at_half]


def one_step(last, core, mine, theirs, b4, w1, w2, counts, sub=8, unroll=8):
    vmem = pl.BlockSpec(memory_space=pltpu.VMEM)
    smem = pl.BlockSpec(memory_space=pltpu.SMEM)
    rows = counts.shape[0]
    kernel = last_kernel if last else middle_kernel
    out = jax.ShapeDtypeStruct(((2 if last else 1) * mine.shape[0], LANES), jnp.float32)
    scratch = [pltpu.VMEM((rows, LANES), jnp.float32)] * 2
    return pl.pallas_call(
        functools.partial(kernel, sub, unroll),
        in_specs=[smem] + [vmem] * 6,
        out_specs=[vmem] * 2,
        out_shape=[out] * 2,
        scratch_shapes=scratch,
        compiler_params=pltpu.CompilerParams(
            vmem_limit_bytes=8 << 20
        ),
    )(core, mine, theirs, b4, w1, w2, counts)


def spread_kernel(mine_ref, theirs_ref, out_ref):
    x = mine_ref[...] + theirs_ref[...]
    for i in range(out_ref.shape[0]):
        out_ref[i] = x


def update_kernel(got_ref, cur_ref, scale_ref, out_ref):
    t = got_ref[0]
    for i in range(1, got_ref.shape[0]):
        t = t + got_ref[i]
    out_ref[...] = cur_ref[...] * (t * scale_ref[...])


def start_kernel(cells, got_ref, mine_ref, theirs_ref, mine_out, theirs_out, scale_out):
    t = got_ref[0]
    for i in range(1, got_ref.shape[0]):
        t = t + got_ref[i]
    scale = (cells / (t * pltpu.roll(t, R, 1)))[:1]
    mine_out[...] = mine_ref[...] * scale
    theirs_out[...] = theirs_ref[...] * scale
    scale_out[...] = scale * (1.0 / cells)


def small(kernel, shapes, *args):
    vmem = pl.BlockSpec(memory_space=pltpu.VMEM)
    return pl.pallas_call(
        kernel,
        in_specs=[vmem] * len(args),
        out_specs=[vmem] * len(shapes),
        out_shape=[jax.ShapeDtypeStruct(shape, jnp.float32) for shape in shapes],
        compiler_params=pltpu.CompilerParams(vmem_limit_bytes=2 << 20),
    )(*args)


AXES = ("col", "tm")
SAME_CORE = [[i for i in range(32) if i // 2 % 2 == core] for core in range(2)]


def send(x, bit):
    return lax.ppermute(x, AXES, [(i, i ^ bit) for i in range(32)])


def per_device(counts, factor_a, factor_b, factor_c):
    col_count = lax.axis_size("col")
    tm_count = lax.axis_size("tm")
    groups = col_count * tm_count
    whole_j = factor_b.shape[0] * groups
    whole_k = factor_c.shape[0] * tm_count
    cells = float(whole_j * whole_k)
    position = lax.axis_index(AXES)
    core = position // 2 % 2
    own = jnp.concatenate(
        [jnp.sum(factor_b, axis=0), jnp.sum(factor_c, axis=0) * (1.0 / col_count)]
    )
    other = send(factor_b, 1)
    first = lax.axis_index("tm") == 0
    b_local = jnp.concatenate(
        [jnp.where(first, factor_b, other), jnp.where(first, other, factor_b)], axis=0
    )
    b4 = jnp.tile(b_local, (1, FOLD))
    c_high, c_low = halves(factor_c)
    none = jnp.zeros_like(c_high)
    w1 = jnp.concatenate([c_high.T, c_low.T, none.T, none.T] * 2, axis=0)
    w2 = jnp.concatenate([c_high, c_low, none, none], axis=1)
    cur = pack(factor_a)
    half = cur.shape[0] // 2
    mine = lax.dynamic_slice_in_dim(cur, core * half, half, 0)
    theirs = lax.dynamic_slice_in_dim(cur, (1 - core) * half, half, 0)
    own = jnp.broadcast_to(jnp.tile(own, 2), (groups, 8, LANES))
    own, mine, theirs, which_core, b4, w1, w2 = lax.optimization_barrier(
        (own, mine, theirs, core.reshape(1), b4, w1, w2)
    )
    own = lax.all_to_all(own, AXES, 0, 0, tiled=True)
    mine, theirs, to_phi = small(
        functools.partial(start_kernel, cells), [mine.shape, mine.shape, (1, LANES)], own, mine, theirs
    )
    for _ in range(ITERS - 1):
        got = one_step(False, which_core, mine, theirs, b4, w1, w2, counts)
        (t,) = small(spread_kernel, [(groups // 2, half, LANES)], got[0], send(got[1], 2))
        t = lax.all_to_all(t, AXES, 0, 0, axis_index_groups=SAME_CORE, tiled=True)
        (mine,) = small(update_kernel, [mine.shape], t, mine, to_phi)
        theirs = send(mine, 2)
    cur, t = one_step(True, which_core, mine, theirs, b4, w1, w2, counts)
    own_rows = counts.shape[0] // groups
    blocks = cur.shape[0] // own_rows
    t = jnp.broadcast_to(
        t.reshape(1, blocks, own_rows, LANES), (groups // blocks, blocks, own_rows, LANES)
    ).reshape(groups, own_rows, LANES)
    t = jnp.sum(lax.all_to_all(t, AXES, 0, 0, tiled=True), axis=0)
    cur = lax.dynamic_slice_in_dim(cur, (position % blocks) * own_rows, own_rows, 0)
    cur = cur * (t * (1.0 / cells))
    return lax.dynamic_slice_in_dim(cur, (position // blocks) * R, R, 1)


def solution(mesh):
    return jax.shard_map(
        per_device,
        mesh=mesh,
        in_specs=(P("row", "col", "tm"), P("row", None), P(("col", "tm"), None), P("tm", None)),
        out_specs=P(("row", "col", "tm"), None),
        check_vma=False,
    )
```
